32 devices in a mesh: wide: 16 (over z, y, x), narrow: 2 (over core).
Axes of the slice: x: 2, y: 2, z: 4, core: 2. Of those that a mesh axis runs over, the one named last changes fastest.
Arguments:
- blocks: float32 [256, 14, 128, 128], P('wide', 'narrow'), may hold values from -0.125 to 0.125
- vectors: float32 [32768, 512], P('wide'), may hold values from -1.5 to 1.5
- sign_bits: int32 [32768], P('wide'), may hold values from 0 to 1
- column_blocks: int32 [256, 14], P('wide', 'narrow'), may hold values from 0 to 255, as said below
- sample_rows: int32 [1024], P('wide'), may hold values from 0 to 32767, as said below
Outputs:
- sketch: float32 [1024, 512], P('wide', 'narrow')
The draws below stay inside these ranges and needn't reach their ends.
Inputs may be any that keep to these rules, and one draw needn't show every extreme that they name: `column_blocks`: entry [g, j] equals (g + o) mod 256 for an offset o with -8 <= o <= 8; both offsets -8 and 8 occur in every draw. `sample_rows`: entries 64 * w to 64 * w + 63 are distinct rows of slab w, that is of rows 16 * 128 * w to 16 * 128 * w + 16 * 128 - 1, in increasing order.
All inputs are finite; a program needn't handle non-finite values.
Results may differ from the reference program's by a relative error of at most 0.00013.
Values sent between devices are 32-bit elements; how exact they have to be, the bound alone decides.
A program may use at most 192 MiB of HBM per device.

```python
import math
import jax
import jax.numpy as jnp
from jax import lax

BLK = 128
NNZB = 14
KCOL = 512
REACH = 8
BR_DEV = 16
S_DEV = 64
NB = 256
NN = 32768
SAMPLES = 1024
N_WIDE = 16


def draw_column_blocks(key, part):
    total_blocks = BR_DEV * N_WIDE
    offsets = jax.random.randint(key, (total_blocks, NNZB), -REACH, REACH + 1, dtype=jnp.int32)
    offsets = offsets.at[0, 0].set(-REACH)
    offsets = offsets.at[total_blocks - 1, 1].set(REACH)
    offsets = offsets.at[0, 2].set(-1)
    offsets = offsets.at[total_blocks - 1, 3].set(1)
    block_rows = jnp.arange(total_blocks, dtype=jnp.int32)[:, None]
    return ((block_rows + offsets) % total_blocks).astype(jnp.int32)


def draw_sample_rows(key, part):
    rows_slab = BR_DEV * BLK
    slab_keys = jax.random.split(key, N_WIDE)

    def one_slab(slab_key):
        return jnp.sort(jax.random.permutation(slab_key, rows_slab)[:S_DEV])
    local_rows = jax.vmap(one_slab)(slab_keys).astype(jnp.int32)
    local_rows = local_rows.at[0, 0].set(0)
    local_rows = local_rows.at[N_WIDE - 1, S_DEV - 1].set(rows_slab - 1)
    slab_starts = (jnp.arange(N_WIDE, dtype=jnp.int32) * rows_slab)[:, None]
    return (local_rows + slab_starts).reshape(-1).astype(jnp.int32)


def place_ends(values, stream_key, least, high):
    spot = [jax.random.randint(jax.random.fold_in(stream_key, axis), (), 0, length) for axis, length in enumerate(values.shape)]
    longest = values.shape.index(max(values.shape))
    next_to = spot[:longest] + [(spot[longest] + 1) % values.shape[longest]] + spot[longest + 1:]
    return values.at[tuple(spot)].set(least).at[tuple(next_to)].set(high)


def level_of(rng, dims, cuts, smallest, largest):
    def one(dim, shards_of):
        steps = jax.random.uniform(jax.random.fold_in(jax.random.fold_in(rng, 6), dim), (shards_of,), jnp.float32, smallest / len(cuts), largest / len(cuts))
        return jnp.repeat(jnp.exp(steps), dims[dim] // shards_of).reshape((-1,) + (1,) * (len(dims) - dim - 1))

    loudness = one(*cuts[0])
    for cut in cuts[1:]:
        loudness = loudness * one(*cut)
    return loudness


def normal_values(stream_key, extent, width, most, cuts=(), kind=jnp.bfloat16):
    level = level_of(stream_key, extent, cuts, -0.22, 0.18) if cuts else 1.0
    values = jax.random.normal(stream_key, extent, jnp.float32) * width * level
    return jnp.minimum(jnp.maximum(values, -most), most).astype(kind)


def setup_inputs(seed: int = 0) -> dict:
    streams_of = jax.random.split(jax.random.key(seed), 6)
    return {
        "blocks": normal_values(streams_of[0], (NB, NNZB, BLK, BLK), (NNZB * BLK) ** -0.5, 0.125, ((0, 16), (1, 2)), jnp.float32),
        "vectors": normal_values(streams_of[1], (NN, KCOL), 0.25, 1.5, ((0, 16),), jnp.float32),
        "sign_bits": place_ends(jax.random.randint(streams_of[2], (NN,), 0, 2), jax.random.fold_in(streams_of[2], 1), 0, 1).astype(jnp.int32),
        "column_blocks": draw_column_blocks(jax.random.fold_in(streams_of[5], 71), 0),
        "sample_rows": draw_sample_rows(jax.random.fold_in(streams_of[5], 71), 0),
    }


def sylvester_matrix(order):
    positions = jnp.arange(order, dtype=jnp.int32)
    common = positions[:, None] & positions[None, :]
    parity = jnp.zeros((order, order), jnp.int32)
    for shift_bits in range(max(order - 1, 1).bit_length()):
        parity = parity + (common >> shift_bits & 1)
    return (1 - 2 * (parity % 2)).astype(jnp.float32)

def reference(blocks, vectors, sign_bits, column_blocks, sample_rows):
    highest = lax.Precision.HIGHEST
    vector_blocks = vectors.reshape(NB, BLK, KCOL)
    slab_blocks = blocks.reshape(N_WIDE, BR_DEV, NNZB, BLK, BLK)
    slab_columns = column_blocks.reshape(N_WIDE, BR_DEV, NNZB)

    def slab_product(pieces):
        block_slab, column_slab = pieces
        picked = vector_blocks[column_slab]
        return jnp.einsum('bjik,bjkn->bin', block_slab, picked, precision=highest)
    product = lax.map(slab_product, (slab_blocks, slab_columns))
    signs = (2 * sign_bits - 1).astype(jnp.float32).reshape(N_WIDE, BR_DEV, BLK, 1)
    signed = product * signs
    local_mix = jnp.einsum('ik,wbkn->wbin', sylvester_matrix(BLK), signed, precision=highest)
    mixed = jnp.einsum('wv,vbin->wbin', sylvester_matrix(N_WIDE), local_mix, precision=highest)
    scale = math.sqrt(NN / SAMPLES) / math.sqrt(BLK * N_WIDE)
    return (mixed.reshape(NN, KCOL) * scale)[sample_rows]
```

```python
import functools
import math

import jax
import jax.numpy as jnp
from jax import lax
from jax.experimental import pallas as pl
from jax.experimental.pallas import tpu as pltpu
from jax.sharding import PartitionSpec as P

REACH = 8
MESH = pl.DeviceIdType.MESH


def split_bf16(x):
    high = x.astype(jnp.bfloat16)
    return high, (x - high.astype(jnp.float32)).astype(jnp.bfloat16)


def sketch_kernel(shares, slots, order, *refs):
    columns = refs[:shares]
    blocks = refs[shares:2 * shares]
    before, inside, after, signs, rows_mix, rows_block, out = refs[2 * shares:2 * shares + 7]
    high, low = refs[2 * shares + 7:]
    b = pl.program_id(0)
    half = high.shape[2]

    @pl.when(b == 0)
    def _():
        out[...] = jnp.zeros_like(out)
        start = 0
        for piece in (before, inside, after):
            def convert(i, carry, piece=piece, start=start):
                h, l = split_bf16(piece[pl.ds(pl.multiple_of(i * order, order), order), :])
                high[start + i] = h
                low[start + i] = l
                return carry
            count = piece.shape[0] // order
            lax.fori_loop(0, count, convert, 0)
            start += count

    total = jnp.zeros((order, half), jnp.float32)
    pairs = [(share, j) for j in range(slots) for share in range(shares)]
    for at in range(0, len(pairs), 2):
        group = pairs[at:at + 2]
        a = jnp.concatenate([blocks[share][0, j] for share, j in group], axis=1)
        a_high, a_low = split_bf16(a)
        where = [columns[share][b, j] for share, j in group]
        v_high = jnp.concatenate([high[w] for w in where], axis=0)
        v_low = jnp.concatenate([low[w] for w in where], axis=0)
        both = jnp.dot(
            jnp.concatenate([a_high, a_low], axis=0), v_high, preferred_element_type=jnp.float32
        )
        small = jnp.dot(a_high, v_low, preferred_element_type=jnp.float32)
        total = total + (both[:order] + (both[order:] + small))
    p_high, p_low = split_bf16(total)
    stacked = jnp.concatenate([p_high, p_low], axis=0)
    sign = (2 * signs[0] - 1).astype(jnp.float32)
    step = min(256, out.shape[0])

    def mix(i, carry):
        rows = pl.ds(pl.multiple_of(i * step, step), step)
        r = jnp.where(rows_block[rows, :] == b, rows_mix[rows, :] * sign, 0.0).astype(jnp.bfloat16)
        out[rows, :] += jnp.dot(
            jnp.concatenate([r, r], axis=1), stacked, preferred_element_type=jnp.float32
        )
        return carry
    lax.fori_loop(0, out.shape[0] // step, mix, 0, unroll=out.shape[0] // step <= 4)


def scatter_kernel(count, scale, x, out, held, send_sem, recv_sem):
    me = lax.axis_index("wide")

    def copy(p):
        to = (me + p) % count
        return pltpu.make_async_remote_copy(
            src_ref=x.at[to],
            dst_ref=held.at[p],
            send_sem=send_sem.at[p],
            recv_sem=recv_sem.at[p],
            device_id={"wide": to},
            device_id_type=MESH,
        )

    def begin(p, carry):
        copy(p).start()
        return carry

    def end(p, carry):
        copy(p).wait()
        out[...] += held[p]
        return carry
    lax.fori_loop(1, count, begin, 0)
    out[...] = x[me]
    lax.fori_loop(1, count, end, 0)
    out[...] = out[...] * scale


def parity_sign(bits):
    return (1 - 2 * (lax.population_count(bits) & 1)).astype(jnp.float32)


def local(blocks, vectors, sign_bits, column_blocks, sample_rows):
    slab_rows, slots, order = blocks.shape[:3]
    width = vectors.shape[1]
    wide_count = lax.axis_size("wide")
    shares = lax.axis_size("narrow")
    half = width // shares
    me = lax.axis_index("wide")
    total_blocks = slab_rows * wide_count
    slab_total = slab_rows * order
    samples_slab = sample_rows.shape[0]
    samples = samples_slab * wide_count

    inside = lax.dynamic_slice_in_dim(vectors, lax.axis_index("narrow") * half, half, axis=1)
    reach_rows = REACH * order
    up = [(i, (i + 1) % wide_count) for i in range(wide_count)]
    down = [(j, i) for i, j in up]
    before = lax.ppermute(inside[slab_total - reach_rows:], "wide", up)
    after = lax.ppermute(inside[:reach_rows], "wide", down)

    local_columns = (column_blocks - me * slab_rows + REACH) % total_blocks
    all_blocks, all_columns = [blocks], [local_columns]
    for shift in range(1, shares):
        pairs = [(i, (i + shift) % shares) for i in range(shares)]
        all_blocks.append(lax.ppermute(blocks, "narrow", pairs))
        all_columns.append(lax.ppermute(local_columns, "narrow", pairs))

    gathered = sample_rows[None]
    reach = 1
    while reach < wide_count:
        pairs = [(i, i ^ reach) for i in range(wide_count)]
        gathered = jnp.concatenate([gathered, lax.ppermute(gathered, "wide", pairs)], axis=0)
        reach *= 2
    order_of = jnp.arange(wide_count, dtype=jnp.int32) ^ me
    picked = jnp.take(gathered, order_of, axis=0).reshape(samples, 1)
    slab_of = picked // slab_total
    inner = picked - slab_of * slab_total
    positions = jnp.arange(order, dtype=jnp.int32)[None]
    rows_mix = parity_sign(positions & inner) * parity_sign(slab_of & me)
    rows_block = jnp.broadcast_to(inner // order, (samples, order))

    def whole(shape):
        return pl.BlockSpec(shape, lambda b, *_: (0,) * len(shape), pipeline_mode=pl.Buffered(1))
    partial = pl.pallas_call(
        functools.partial(sketch_kernel, shares, slots, order),
        grid_spec=pltpu.PrefetchScalarGridSpec(
            num_scalar_prefetch=shares,
            grid=(slab_rows,),
            in_specs=[
                pl.BlockSpec((1, slots, order, order), lambda b, *_: (b, 0, 0, 0))
                for _ in range(shares)
            ] + [
                whole((reach_rows, half)),
                whole((slab_total, half)),
                whole((reach_rows, half)),
                pl.BlockSpec((1, 1, order), lambda b, *_: (b, 0, 0)),
                whole((samples, order)),
                whole((samples, order)),
            ],
            out_specs=pl.BlockSpec((samples, half), lambda b, *_: (0, 0)),
            scratch_shapes=[
                pltpu.VMEM((slab_rows + 2 * REACH, order, half), jnp.bfloat16),
                pltpu.VMEM((slab_rows + 2 * REACH, order, half), jnp.bfloat16),
            ],
        ),
        out_shape=jax.ShapeDtypeStruct((samples, half), jnp.float32),
        name="sketch",
    )(*all_columns, *all_blocks, before, inside, after,
      sign_bits.reshape(slab_rows, 1, order), rows_mix, rows_block)

    scale = math.sqrt(slab_total * wide_count / samples) / math.sqrt(order * wide_count)
    return pl.pallas_call(
        functools.partial(scatter_kernel, wide_count, scale),
        in_specs=[pl.BlockSpec(memory_space=pltpu.VMEM)],
        out_specs=pl.BlockSpec(memory_space=pltpu.VMEM),
        out_shape=jax.ShapeDtypeStruct((samples_slab, half), jnp.float32),
        scratch_shapes=[
            pltpu.VMEM((wide_count, samples_slab, half), jnp.float32),
            pltpu.SemaphoreType.DMA((wide_count,)),
            pltpu.SemaphoreType.DMA((wide_count,)),
        ],
        compiler_params=pltpu.CompilerParams(has_side_effects=True),
        name="scatter",
    )(partial.reshape(wide_count, samples_slab, half))


def solution(mesh):
    return jax.shard_map(
        local,
        mesh=mesh,
        in_specs=(
            P("wide", "narrow", None, None),
            P("wide", None),
            P("wide"),
            P("wide", "narrow"),
            P("wide"),
        ),
        out_specs=P("wide", "narrow"),
        check_vma=False,
    )
```

```python
import functools
import math

import jax
import jax.numpy as jnp
from jax import lax
from jax.experimental import pallas as pl
from jax.experimental.pallas import tpu as pltpu
from jax.sharding import PartitionSpec as P

REACH = 8
MESH = pl.DeviceIdType.MESH


def split_bf16(x):
    high = x.astype(jnp.bfloat16)
    return high, (x - high.astype(jnp.float32)).astype(jnp.bfloat16)


def add_pairs(first, last, b, r, slots, order, which, columns, blocks, high, low, shift, total):
    def block(at):
        which_at = which[b, at]
        found = blocks[0][r, which_at % slots]
        for share in range(1, len(blocks)):
            found = jnp.where(which_at // slots == share, blocks[share][r, which_at % slots], found)
        return found

    def pair(i, carry):
        one = first + 2 * i
        two = jnp.minimum(one + 1, last - 1)
        kept = (one + 1 < last).astype(jnp.float32)
        a = jnp.concatenate([block(one), block(two) * kept], axis=1)
        a_high, a_low = split_bf16(a)
        where = [shift(columns[b, at]) for at in (one, two)]
        v_high = jnp.concatenate([high[w] for w in where], axis=0)
        v_low = jnp.concatenate([low[w] for w in where], axis=0)
        both = jnp.dot(
            jnp.concatenate([a_high, a_low], axis=0), v_high, preferred_element_type=jnp.float32
        )
        small = jnp.dot(a_high, v_low, preferred_element_type=jnp.float32)
        total[...] += both[:order] + (both[order:] + small)
        return carry
    lax.fori_loop(0, (last - first + 1) // 2, pair, 0)


def convert_rows(piece, start, order, high, low):
    def convert(i, carry):
        h, l = split_bf16(piece[pl.ds(pl.multiple_of(i * order, order), order), :])
        high[start + i] = h
        low[start + i] = l
        return carry
    lax.fori_loop(0, piece.shape[0] // order, convert, 0)


def inside_kernel(shares, slots, order, which, columns, near, place, *refs):
    blocks, (inside, out, high, low) = refs[:shares], refs[shares:]
    step_rows = blocks[0].shape[0]
    step = pl.program_id(0)

    @pl.when(step == 0)
    def _():
        convert_rows(inside, 0, order, high, low)
    out[...] = jnp.zeros_like(out)

    def row(r, carry):
        b = step * step_rows + r
        add_pairs(
            0, near[b], b, r, slots, order, which, columns, blocks, high, low,
            lambda c: c - REACH, out.at[pl.ds(pl.multiple_of(r * order, order), order), :]
        )
        return carry
    lax.fori_loop(0, step_rows, row, 0)


def sketch_kernel(shares, slots, order, which, columns, near, rows, row_signs, *refs):
    blocks = refs[:shares]
    before, after, product, signs, hadamard, out, high, low, total, mixed = refs[shares:]
    step_rows = blocks[0].shape[0]
    slab_rows = signs.shape[0]
    step = pl.program_id(0)

    @pl.when(step == 0)
    def _():
        convert_rows(before, 0, order, high, low)
        convert_rows(after, REACH, order, high, low)

    def row(r, carry):
        b = step * step_rows + r
        total[...] = product[pl.ds(pl.multiple_of(r * order, order), order), :]
        add_pairs(
            near[b], which.shape[1], b, r, slots, order, which, columns, blocks, high, low,
            lambda c: jnp.where(c < REACH, c, c - slab_rows), total
        )
        stacked = jnp.concatenate(split_bf16(total[...]), axis=0)
        mix = (hadamard[...] * (2 * signs[b] - 1).astype(jnp.float32)).astype(jnp.bfloat16)
        mixed[pl.ds(pl.multiple_of(b * order, order), order), :] = jnp.dot(
            jnp.concatenate([mix, mix], axis=1), stacked, preferred_element_type=jnp.float32
        )
        return carry
    lax.fori_loop(0, step_rows, row, 0)

    @pl.when(step == pl.num_programs(0) - 1)
    def _():
        per_slab = out.shape[0] // row_signs.shape[0]
        group = 8

        def pick(i, carry):
            first = i * group
            sign = row_signs[first // per_slab]
            picked = [mixed[pl.ds(rows[first + k], 1), :] for k in range(group)]
            out[pl.ds(pl.multiple_of(first, group), group), :] = jnp.concatenate(picked, axis=0) * sign
            return carry
        lax.fori_loop(0, out.shape[0] // group, pick, 0, unroll=4)


def scatter_kernel(scale, x, out, held, total, last, send_sem, recv_sem, send_last, recv_last):
    far_count, near_count = x.shape[:2]
    me = lax.axis_index("wide")
    far_me, near_me = me // near_count, me % near_count

    def near_copy(p):
        to = (near_me + p) % near_count
        return pltpu.make_async_remote_copy(
            src_ref=x.at[:, to],
            dst_ref=held.at[p],
            send_sem=send_sem.at[p],
            recv_sem=recv_sem.at[p],
            device_id={"wide": far_me * near_count + to},
            device_id_type=MESH,
        )

    def far_copy(p):
        to = (far_me + p) % far_count
        return pltpu.make_async_remote_copy(
            src_ref=total.at[to],
            dst_ref=last.at[p],
            send_sem=send_last.at[p],
            recv_sem=recv_last.at[p],
            device_id={"wide": to * near_count + near_me},
            device_id_type=MESH,
        )

    def begin(copy):
        def body(p, carry):
            copy(p).start()
            return carry
        return body

    def end_near(p, carry):
        near_copy(p).wait()
        total[...] += held[p]
        return carry

    def end_far(p, carry):
        far_copy(p).wait()
        out[...] += last[p]
        return carry
    lax.fori_loop(1, near_count, begin(near_copy), 0)
    total[...] = x[:, near_me]
    lax.fori_loop(1, near_count, end_near, 0)
    lax.fori_loop(1, far_count, begin(far_copy), 0)
    out[...] = total[far_me]
    lax.fori_loop(1, far_count, end_far, 0)
    out[...] = out[...] * scale


def parity_sign(bits):
    return (1 - 2 * (lax.population_count(bits) & 1)).astype(jnp.float32)


def local(blocks, vectors, sign_bits, column_blocks, sample_rows):
    slab_rows, slots, order = blocks.shape[:3]
    width = vectors.shape[1]
    wide_count = lax.axis_size("wide")
    shares = lax.axis_size("narrow")
    half = width // shares
    me = lax.axis_index("wide")
    total_blocks = slab_rows * wide_count
    slab_total = slab_rows * order
    samples_slab = sample_rows.shape[0]
    samples = samples_slab * wide_count

    def widen(gathered, reach):
        radix = min(4, wide_count // reach)
        parts = [gathered]
        for k in range(1, radix):
            pairs = [(i, i ^ (k * reach)) for i in range(wide_count)]
            parts.append(lax.ppermute(gathered, "wide", pairs))
        return jnp.concatenate(parts, axis=0), reach * radix
    gathered, reach = widen(sample_rows[None], 1)
    narrow_me = lax.axis_index("narrow")
    reach_rows = REACH * order
    up = [(i, (i + 1) % wide_count) for i in range(wide_count)]
    down = [(j, i) for i, j in up]
    last_rows = lax.dynamic_slice(
        vectors, (slab_total - reach_rows, narrow_me * half), (reach_rows, half)
    )
    first_rows = lax.dynamic_slice(vectors, (0, narrow_me * half), (reach_rows, half))
    before = lax.ppermute(last_rows, "wide", up)
    after = lax.ppermute(first_rows, "wide", down)

    local_columns = (column_blocks - me * slab_rows + REACH) % total_blocks
    all_blocks, all_columns = [blocks], [local_columns]
    for shift in range(1, shares):
        pairs = [(i, (i + shift) % shares) for i in range(shares)]
        all_blocks.append(lax.ppermute(blocks, "narrow", pairs))
        all_columns.append(lax.ppermute(local_columns, "narrow", pairs))
    columns = jnp.concatenate(all_columns, axis=1)

    entries = shares * slots
    inside = ((columns >= REACH) & (columns < REACH + slab_rows)).astype(jnp.int32)
    places = jnp.arange(entries, dtype=jnp.int32)
    ahead = (places[None, :] < places[:, None]).astype(jnp.int32)[None]
    near = jnp.sum(inside, axis=1)
    rank = jnp.where(
        inside == 1,
        jnp.sum(inside[:, None, :] * ahead, axis=2),
        near[:, None] + jnp.sum((1 - inside)[:, None, :] * ahead, axis=2),
    )
    chosen = (rank[:, None, :] == places[None, :, None]).astype(jnp.int32)
    which = jnp.sum(chosen * places[None, None, :], axis=2)
    columns = jnp.sum(chosen * columns[:, None, :], axis=2)

    positions = jnp.arange(order, dtype=jnp.int32)
    hadamard = parity_sign(positions[:, None] & positions[None, :])

    def whole(shape):
        return pl.BlockSpec(shape, lambda b, *_: (0,) * len(shape), pipeline_mode=pl.Buffered(1))
    step_rows = math.gcd(slab_rows, 4)
    block_specs = [
        pl.BlockSpec((step_rows, slots, order, order), lambda b, *_: (b, 0, 0, 0))
        for _ in range(shares)
    ]
    row_spec = pl.BlockSpec((step_rows * order, half), lambda b, *_: (b, 0))
    flops = 2 * slab_rows * entries * order * order * half
    product = pl.pallas_call(
        functools.partial(inside_kernel, shares, slots, order),
        grid_spec=pltpu.PrefetchScalarGridSpec(
            num_scalar_prefetch=4,
            grid=(slab_rows // step_rows,),
            in_specs=block_specs + [
                pl.BlockSpec((slab_total, half), lambda b, *s: (0, s[3][0]), pipeline_mode=pl.Buffered(1))
            ],
            out_specs=row_spec,
            scratch_shapes=[pltpu.VMEM((slab_rows, order, half), jnp.bfloat16)] * 2,
        ),
        out_shape=jax.ShapeDtypeStruct((slab_total, half), jnp.float32),
        cost_estimate=pl.CostEstimate(flops=6 * flops, bytes_accessed=20 << 20, transcendentals=0),
        name="inside",
    )(which, columns, near, narrow_me.astype(jnp.int32).reshape(1), *all_blocks, vectors)
    gathered, product = lax.optimization_barrier((gathered, product))
    while reach < wide_count:
        gathered, reach = widen(gathered, reach)
    slabs = jnp.arange(wide_count, dtype=jnp.int32)
    rows = jnp.take(gathered, slabs ^ me, axis=0).reshape(samples) % slab_total
    row_signs = parity_sign(slabs & me)
    partial = pl.pallas_call(
        functools.partial(sketch_kernel, shares, slots, order),
        grid_spec=pltpu.PrefetchScalarGridSpec(
            num_scalar_prefetch=5,
            grid=(slab_rows // step_rows,),
            in_specs=block_specs + [
                whole((reach_rows, half)),
                whole((reach_rows, half)),
                row_spec,
                whole((slab_rows, 1, order)),
                whole((order, order)),
            ],
            out_specs=pl.BlockSpec((samples, half), lambda b, *_: (0, 0)),
            scratch_shapes=[
                pltpu.VMEM((2 * REACH, order, half), jnp.bfloat16),
                pltpu.VMEM((2 * REACH, order, half), jnp.bfloat16),
                pltpu.VMEM((order, half), jnp.float32),
                pltpu.VMEM((slab_total, half), jnp.float32),
            ],
        ),
        out_shape=jax.ShapeDtypeStruct((samples, half), jnp.float32),
        cost_estimate=pl.CostEstimate(flops=2 * flops, bytes_accessed=20 << 20, transcendentals=0),
        name="sketch",
    )(which, columns, near, rows, row_signs, *all_blocks, before, after, product,
      sign_bits.reshape(slab_rows, 1, order), hadamard)

    scale = math.sqrt(slab_total * wide_count / samples) / math.sqrt(order * wide_count)
    near_count = 1 << ((wide_count.bit_length() - 1) // 2)
    far_count = wide_count // near_count
    return pl.pallas_call(
        functools.partial(scatter_kernel, scale),
        in_specs=[pl.BlockSpec(memory_space=pltpu.VMEM)],
        out_specs=pl.BlockSpec(memory_space=pltpu.VMEM),
        out_shape=jax.ShapeDtypeStruct((samples_slab, half), jnp.float32),
        scratch_shapes=[
            pltpu.VMEM((near_count, far_count, samples_slab, half), jnp.float32),
            pltpu.VMEM((far_count, samples_slab, half), jnp.float32),
            pltpu.VMEM((far_count, samples_slab, half), jnp.float32),
            pltpu.SemaphoreType.DMA((near_count,)),
            pltpu.SemaphoreType.DMA((near_count,)),
            pltpu.SemaphoreType.DMA((far_count,)),
            pltpu.SemaphoreType.DMA((far_count,)),
        ],
        compiler_params=pltpu.CompilerParams(has_side_effects=True),
        name="scatter",
    )(partial.reshape(far_count, near_count, samples_slab, half))


def solution(mesh):
    return jax.shard_map(
        local,
        mesh=mesh,
        in_specs=(
            P("wide", "narrow", None, None),
            P("wide", None),
            P("wide"),
            P("wide", "narrow"),
            P("wide"),
        ),
        out_specs=P("wide", "narrow"),
        check_vma=False,
    )
```

```python
import functools
import math

import jax
import jax.numpy as jnp
from jax import lax
from jax.experimental import pallas as pl
from jax.experimental.pallas import tpu as pltpu
from jax.sharding import PartitionSpec as P

REACH = 8
MESH = pl.DeviceIdType.MESH


def split_bf16(x):
    high = x.astype(jnp.bfloat16)
    return high, (x - high.astype(jnp.float32)).astype(jnp.bfloat16)


def add_pairs(first, last, b, r, slots, order, which, columns, blocks, high, low, shift, total):
    def block(at):
        which_at = which[b, at]
        found = blocks[0][r, which_at % slots]
        for share in range(1, len(blocks)):
            found = jnp.where(which_at // slots == share, blocks[share][r, which_at % slots], found)
        return found

    group = 4

    def several(i, carry):
        parts = []
        for at in range(0, group, 2):
            entries = [first + group * i + at + k for k in range(2)]
            found = [jnp.minimum(e, last - 1) for e in entries]
            a = jnp.concatenate(
                [block(f) * (e < last).astype(jnp.float32) for e, f in zip(entries, found)], axis=1
            )
            a_high, a_low = split_bf16(a)
            where = [shift(columns[b, f]) for f in found]
            v_high = jnp.concatenate([high[w] for w in where], axis=0)
            v_low = jnp.concatenate([low[w] for w in where], axis=0)
            both = jnp.dot(
                jnp.concatenate([a_high, a_low], axis=0), v_high, preferred_element_type=jnp.float32
            )
            small = jnp.dot(a_high, v_low, preferred_element_type=jnp.float32)
            parts.append(both[:order] + (both[order:] + small))
        total[...] += functools.reduce(jnp.add, parts)
        return carry
    lax.fori_loop(0, (last - first + group - 1) // group, several, 0)


def convert_rows(piece, start, order, high, low):
    def convert(i, carry):
        h, l = split_bf16(piece[pl.ds(pl.multiple_of(i * order, order), order), :])
        high[start + i] = h
        low[start + i] = l
        return carry
    lax.fori_loop(0, piece.shape[0] // order, convert, 0)


def inside_kernel(shares, slots, order, which, columns, near, place, *refs):
    blocks, (inside, out, high, low) = refs[:shares], refs[shares:]
    step_rows = blocks[0].shape[0]
    step = pl.program_id(0)

    @pl.when(step == 0)
    def _():
        convert_rows(inside, 0, order, high, low)
    out[...] = jnp.zeros_like(out)

    def row(r, carry):
        b = step * step_rows + r
        add_pairs(
            0, near[b], b, r, slots, order, which, columns, blocks, high, low,
            lambda c: c - REACH, out.at[pl.ds(pl.multiple_of(r * order, order), order), :]
        )
        return carry
    lax.fori_loop(0, step_rows, row, 0)


def sketch_kernel(shares, slots, order, which, columns, near, rows, row_signs, *refs):
    blocks = refs[:shares]
    before, after, product, signs, hadamard, out, high, low, total, mixed = refs[shares:]
    step_rows = blocks[0].shape[0]
    slab_rows = signs.shape[0]
    step = pl.program_id(0)

    @pl.when(step == 0)
    def _():
        convert_rows(before, 0, order, high, low)
        convert_rows(after, REACH, order, high, low)

    def row(r, carry):
        b = step * step_rows + r
        total[...] = product[pl.ds(pl.multiple_of(r * order, order), order), :]
        add_pairs(
            near[b], which.shape[1], b, r, slots, order, which, columns, blocks, high, low,
            lambda c: jnp.where(c < REACH, c, c - slab_rows), total
        )
        stacked = jnp.concatenate(split_bf16(total[...]), axis=0)
        mix = (hadamard[...] * (2 * signs[b] - 1).astype(jnp.float32)).astype(jnp.bfloat16)
        mixed[pl.ds(pl.multiple_of(b * order, order), order), :] = jnp.dot(
            jnp.concatenate([mix, mix], axis=1), stacked, preferred_element_type=jnp.float32
        )
        return carry
    lax.fori_loop(0, step_rows, row, 0)

    @pl.when(step == pl.num_programs(0) - 1)
    def _():
        per_slab = out.shape[0] // row_signs.shape[0]
        group = 8

        def pick(i, carry):
            first = i * group
            sign = row_signs[first // per_slab]
            picked = [mixed[pl.ds(rows[first + k], 1), :] for k in range(group)]
            out[pl.ds(pl.multiple_of(first, group), group), :] = jnp.concatenate(picked, axis=0) * sign
            return carry
        lax.fori_loop(0, out.shape[0] // group, pick, 0, unroll=4)


def scatter_kernel(scale, x, out, held, total, last, send_sem, recv_sem, send_last, recv_last):
    far_count, near_count = x.shape[:2]
    me = lax.axis_index("wide")
    far_me, near_me = me // near_count, me % near_count

    def near_copy(p):
        to = (near_me + p) % near_count
        return pltpu.make_async_remote_copy(
            src_ref=x.at[:, to],
            dst_ref=held.at[p],
            send_sem=send_sem.at[p],
            recv_sem=recv_sem.at[p],
            device_id={"wide": far_me * near_count + to},
            device_id_type=MESH,
        )

    def far_copy(p):
        to = (far_me + p) % far_count
        return pltpu.make_async_remote_copy(
            src_ref=total.at[to],
            dst_ref=last.at[p],
            send_sem=send_last.at[p],
            recv_sem=recv_last.at[p],
            device_id={"wide": to * near_count + near_me},
            device_id_type=MESH,
        )

    def begin(copy):
        def body(p, carry):
            copy(p).start()
            return carry
        return body

    def end_near(p, carry):
        near_copy(p).wait()
        total[...] += held[p]
        return carry

    def end_far(p, carry):
        far_copy(p).wait()
        out[...] += last[p]
        return carry
    lax.fori_loop(1, near_count, begin(near_copy), 0)
    total[...] = x[:, near_me]
    lax.fori_loop(1, near_count, end_near, 0)
    lax.fori_loop(1, far_count, begin(far_copy), 0)
    out[...] = total[far_me]
    lax.fori_loop(1, far_count, end_far, 0)
    out[...] = out[...] * scale


def parity_sign(bits):
    return (1 - 2 * (lax.population_count(bits) & 1)).astype(jnp.float32)


def local(blocks, vectors, sign_bits, column_blocks, sample_rows):
    slab_rows, slots, order = blocks.shape[:3]
    width = vectors.shape[1]
    wide_count = lax.axis_size("wide")
    shares = lax.axis_size("narrow")
    half = width // shares
    me = lax.axis_index("wide")
    total_blocks = slab_rows * wide_count
    slab_total = slab_rows * order
    samples_slab = sample_rows.shape[0]
    samples = samples_slab * wide_count

    def widen(gathered, reach):
        radix = min(4, wide_count // reach)
        parts = [gathered]
        for k in range(1, radix):
            pairs = [(i, i ^ (k * reach)) for i in range(wide_count)]
            parts.append(lax.ppermute(gathered, "wide", pairs))
        return jnp.concatenate(parts, axis=0), reach * radix
    gathered, reach = widen(sample_rows[None], 1)
    narrow_me = lax.axis_index("narrow")
    reach_rows = REACH * order
    up = [(i, (i + 1) % wide_count) for i in range(wide_count)]
    down = [(j, i) for i, j in up]
    last_rows = lax.dynamic_slice(
        vectors, (slab_total - reach_rows, narrow_me * half), (reach_rows, half)
    )
    first_rows = lax.dynamic_slice(vectors, (0, narrow_me * half), (reach_rows, half))
    before = lax.ppermute(last_rows, "wide", up)
    after = lax.ppermute(first_rows, "wide", down)

    local_columns = (column_blocks - me * slab_rows + REACH) % total_blocks
    all_blocks, all_columns = [blocks], [local_columns]
    for shift in range(1, shares):
        pairs = [(i, (i + shift) % shares) for i in range(shares)]
        all_blocks.append(lax.ppermute(blocks, "narrow", pairs))
        all_columns.append(lax.ppermute(local_columns, "narrow", pairs))
    columns = jnp.concatenate(all_columns, axis=1)

    entries = shares * slots
    inside = ((columns >= REACH) & (columns < REACH + slab_rows)).astype(jnp.int32)
    places = jnp.arange(entries, dtype=jnp.int32)
    ahead = (places[None, :] < places[:, None]).astype(jnp.int32)[None]
    near = jnp.sum(inside, axis=1)
    rank = jnp.where(
        inside == 1,
        jnp.sum(inside[:, None, :] * ahead, axis=2),
        near[:, None] + jnp.sum((1 - inside)[:, None, :] * ahead, axis=2),
    )
    chosen = (rank[:, None, :] == places[None, :, None]).astype(jnp.int32)
    which = jnp.sum(chosen * places[None, None, :], axis=2)
    columns = jnp.sum(chosen * columns[:, None, :], axis=2)

    positions = jnp.arange(order, dtype=jnp.int32)
    hadamard = parity_sign(positions[:, None] & positions[None, :])

    def whole(shape):
        return pl.BlockSpec(shape, lambda b, *_: (0,) * len(shape), pipeline_mode=pl.Buffered(1))
    step_rows = math.gcd(slab_rows, 4)
    block_specs = [
        pl.BlockSpec((step_rows, slots, order, order), lambda b, *_: (b, 0, 0, 0))
        for _ in range(shares)
    ]
    row_spec = pl.BlockSpec((step_rows * order, half), lambda b, *_: (b, 0))
    flops = 2 * slab_rows * entries * order * order * half
    product = pl.pallas_call(
        functools.partial(inside_kernel, shares, slots, order),
        grid_spec=pltpu.PrefetchScalarGridSpec(
            num_scalar_prefetch=4,
            grid=(slab_rows // step_rows,),
            in_specs=block_specs + [
                pl.BlockSpec((slab_total, half), lambda b, *s: (0, s[3][0]), pipeline_mode=pl.Buffered(1))
            ],
            out_specs=row_spec,
            scratch_shapes=[pltpu.VMEM((slab_rows, order, half), jnp.bfloat16)] * 2,
        ),
        out_shape=jax.ShapeDtypeStruct((slab_total, half), jnp.float32),
        cost_estimate=pl.CostEstimate(flops=6 * flops, bytes_accessed=20 << 20, transcendentals=0),
        name="inside",
    )(which, columns, near, narrow_me.astype(jnp.int32).reshape(1), *all_blocks, vectors)
    gathered, product = lax.optimization_barrier((gathered, product))
    while reach < wide_count:
        gathered, reach = widen(gathered, reach)
    slabs = jnp.arange(wide_count, dtype=jnp.int32)
    rows = jnp.take(gathered, slabs ^ me, axis=0).reshape(samples) % slab_total
    row_signs = parity_sign(slabs & me)
    partial = pl.pallas_call(
        functools.partial(sketch_kernel, shares, slots, order),
        grid_spec=pltpu.PrefetchScalarGridSpec(
            num_scalar_prefetch=5,
            grid=(slab_rows // step_rows,),
            in_specs=block_specs + [
                whole((reach_rows, half)),
                whole((reach_rows, half)),
                row_spec,
                whole((slab_rows, 1, order)),
                whole((order, order)),
            ],
            out_specs=pl.BlockSpec((samples, half), lambda b, *_: (0, 0)),
            scratch_shapes=[
                pltpu.VMEM((2 * REACH, order, half), jnp.bfloat16),
                pltpu.VMEM((2 * REACH, order, half), jnp.bfloat16),
                pltpu.VMEM((order, half), jnp.float32),
                pltpu.VMEM((slab_total, half), jnp.float32),
            ],
        ),
        out_shape=jax.ShapeDtypeStruct((samples, half), jnp.float32),
        cost_estimate=pl.CostEstimate(flops=2 * flops, bytes_accessed=20 << 20, transcendentals=0),
        name="sketch",
    )(which, columns, near, rows, row_signs, *all_blocks, before, after, product,
      sign_bits.reshape(slab_rows, 1, order), hadamard)

    scale = math.sqrt(slab_total * wide_count / samples) / math.sqrt(order * wide_count)
    near_count = 1 << ((wide_count.bit_length() - 1) // 2)
    far_count = wide_count // near_count
    return pl.pallas_call(
        functools.partial(scatter_kernel, scale),
        in_specs=[pl.BlockSpec(memory_space=pltpu.VMEM)],
        out_specs=pl.BlockSpec(memory_space=pltpu.VMEM),
        out_shape=jax.ShapeDtypeStruct((samples_slab, half), jnp.float32),
        scratch_shapes=[
            pltpu.VMEM((near_count, far_count, samples_slab, half), jnp.float32),
            pltpu.VMEM((far_count, samples_slab, half), jnp.float32),
            pltpu.VMEM((far_count, samples_slab, half), jnp.float32),
            pltpu.SemaphoreType.DMA((near_count,)),
            pltpu.SemaphoreType.DMA((near_count,)),
            pltpu.SemaphoreType.DMA((far_count,)),
            pltpu.SemaphoreType.DMA((far_count,)),
        ],
        compiler_params=pltpu.CompilerParams(has_side_effects=True),
        name="scatter",
    )(partial.reshape(far_count, near_count, samples_slab, half))


def solution(mesh):
    return jax.shard_map(
        local,
        mesh=mesh,
        in_specs=(
            P("wide", "narrow", None, None),
            P("wide", None),
            P("wide"),
            P("wide", "narrow"),
            P("wide"),
        ),
        out_specs=P("wide", "narrow"),
        check_vma=False,
    )
```
